128 devices in a mesh: row: 16 (over z, y), col: 8 (over x, core).
Axes of the slice: x: 4, y: 4, z: 4, core: 2. Of those that a mesh axis runs over, the one named last changes fastest.
Arguments:
- amplitudes: bfloat16 [16, 4, 1024, 1024], P(None, None, 'row', 'col'), may hold values from -6 to 6
- cycle_integrals: bfloat16 [4, 8, 1024, 1024], P(None, None, 'row', 'col'), may hold values from -0.375 to 0.375
- mask_amp: int32 [16, 16], replicated, may hold values 0 or 1
- mask_int: int32 [16, 16], replicated, may hold values 0 or 1
- occupied_i: float32 [16], P('row'), may hold values from -1 to -0.3
- occupied_j: float32 [8], P('col'), may hold values from -1 to -0.3
- virtual_energy: float32 [1024], replicated, may hold values from 0.2 to 1.5
Outputs:
- update: bfloat16 [16, 8, 1024, 1024], P('row', 'col')
The draws below stay inside these ranges and needn't reach their ends.
Inputs may be any that keep to these rules, and one draw needn't show every extreme that they name: mask_amp holds 0 or 1: 1 where the amplitude tile survives screening. mask_int holds 0 or 1: 1 where the intermediate tile survives screening.
All inputs are finite; a program needn't handle non-finite values.
Results may differ from the reference program's by a relative error of at most 0.0049.
Values may be sent and summed in bfloat16 or wider, within the bound.
A program may use at most 192 MiB of HBM per device.

```python
import jax
import jax.numpy as jnp
from jax import lax

TILE = 64
NVT = 16
OK = 4
NV = 1024
OI = 16
OJ = 8


def with_ends(entries, stream_key, smallest, largest):
    shape = entries.shape
    place = [jax.random.randint(jax.random.fold_in(stream_key, axis), (), 0, shape[axis]) for axis in range(len(shape))]
    entries = entries.at[tuple(place)].set(smallest)
    longest = shape.index(max(shape))
    place[longest] = (place[longest] + 1) % shape[longest]
    return entries.at[tuple(place)].set(largest)


def strengthened(result, rng, source, target, shards_of, factor):
    owner, partner = [(jnp.arange(result.shape[axis_at]) // (result.shape[axis_at] // shards_of)).reshape([-1 if axis == axis_at else 1 for axis in range(result.ndim)]) for axis_at in (source, target)]
    chosen = jax.random.permutation(rng, shards_of)[partner]
    strong = (owner == chosen) | (owner == (partner + shards_of // 2) % shards_of)
    return jnp.where(strong, factor * result, result)


def block_scale(rng, extent, shards, least, top_value):
    loudness = 1.0
    for dim, parts in shards:
        heights = jax.random.uniform(jax.random.fold_in(jax.random.fold_in(rng, 6), dim), (parts,), jnp.float32, least / len(shards), top_value / len(shards))
        loudness = loudness * jnp.repeat(jnp.exp(heights), extent[dim] // parts).reshape((-1,) + (1,) * (len(extent) - 1 - dim))
    return loudness


def bell_draw(key, dims, width, most, cuts=(), dtype=jnp.bfloat16):
    values = jax.random.normal(key, dims, jnp.float32) * width
    if len(cuts) > 0:
        values = block_scale(key, dims, cuts, -0.22, 0.18) * values
    return jnp.clip(values, min=-most, max=most).astype(dtype)


def bell_draw_with(stream_key, extent, deviation, bound, cuts, heavy, held_as=jnp.bfloat16):
    entries = deviation * jax.random.normal(stream_key, extent, jnp.float32)
    if cuts:
        entries = entries * block_scale(stream_key, extent, cuts, -0.22, 0.18)
    return jnp.clip(strengthened(entries, jax.random.fold_in(stream_key, 3), *heavy), -bound, bound).astype(held_as)


def setup_inputs(seed: int = 0) -> dict:
    streams_of = jax.random.split(jax.random.key(seed), 8)
    return {
        "amplitudes": bell_draw(streams_of[0], (OI, OK, NV, NV), 1.0, 6.0, ((2, 16), (3, 8))),
        "cycle_integrals": bell_draw_with(streams_of[1], (OK, OJ, NV, NV), (OK * TILE * 2) ** -0.5, 0.375, ((2, 16), (3, 8)), (3, 1, 8, 2.0)),
        "mask_amp": with_ends((jax.random.randint(streams_of[2], (NVT, NVT), 0, 10) < 3).astype(jnp.int32), jax.random.fold_in(streams_of[2], 1), 0, 1),
        "mask_int": with_ends((jax.random.randint(streams_of[3], (NVT, NVT), 0, 10) < 3).astype(jnp.int32), jax.random.fold_in(streams_of[3], 1), 0, 1),
        "occupied_i": jnp.clip(-1.0 + 0.7 * jax.random.uniform(streams_of[4], (OI,), jnp.float32) ** block_scale(streams_of[4], (OI,), ((0, 16),), -0.2, 0.2), -1.0, -0.3),
        "occupied_j": jnp.clip(-1.0 + 0.7 * jax.random.uniform(streams_of[5], (OJ,), jnp.float32) ** block_scale(streams_of[5], (OJ,), ((0, 8),), -0.2, 0.2), -1.0, -0.3),
        "virtual_energy": jnp.clip(jax.random.uniform(streams_of[6], (NV,), jnp.float32, 0.2, 1.5), 0.2, 1.5),
    }


def expand_mask(mask):
    return jnp.repeat(jnp.repeat(mask, TILE, axis=0), TILE, axis=1)


def reference(amplitudes, cycle_integrals, mask_amp, mask_int, occupied_i, occupied_j, virtual_energy):
    amp_mask = expand_mask(mask_amp).astype(jnp.bfloat16)
    int_mask = expand_mask(mask_int).astype(jnp.bfloat16)
    integrals = (cycle_integrals * int_mask[None, None]).astype(jnp.float32)

    def one_orbital(inputs):
        amp_block, energy_i = inputs
        masked = (amp_block * amp_mask[None]).astype(jnp.float32)
        cycle = jnp.einsum("kac,kjbc->jab", masked, integrals).astype(jnp.bfloat16)
        denominator = virtual_energy[None, :, None] + virtual_energy[None, None, :] - energy_i - occupied_j[:, None, None]
        return (cycle.astype(jnp.float32) / denominator).astype(jnp.bfloat16)

    return lax.map(one_orbital, (amplitudes, occupied_i))
```

```python
import functools

import jax
import jax.numpy as jnp
from jax import lax
from jax.experimental import pallas as pl
from jax.experimental.pallas import tpu as pltpu
from jax.sharding import PartitionSpec as P

TILE = 64
MESH = pl.DeviceIdType.MESH

LEVELS = ((9, 24), (10, 28), (12, 36), (16, 64))


def comm_kernel(
    cap1, cap2, tab, amp, integ, out,
    recv_a, recv_b, grp_b1, ga0, ga1, ga2, ga3, gb0, gb1, gb2, gb3, dense_a, dense_b, acc,
    a1_send, a1_recv, b1_send, b1_recv, ring_send, ring_recv, sib_send, sib_recv,
):
    grp_a, grp_b = (ga0, ga1, ga2, ga3), (gb0, gb1, gb2, gb3)
    row = lax.axis_index("row")
    col = lax.axis_index("col")
    x = col // 2
    core = col % 2
    z = row // 4
    y = row % 4
    p = (1 - core) * y + core * z
    q = (1 - core) * z + core * y
    sp = (1 - core) + core * 4
    sq = (1 - core) * 4 + core

    def row_of(pp, qq):
        return pp * sp + qq * sq

    sibling = (row, 2 * x + 1 - core)

    barrier = pltpu.get_barrier_semaphore()

    def signal(target):
        pl.semaphore_signal(barrier, inc=1, device_id=target, device_id_type=MESH)

    for d in range(1, 16):
        for cc in range(2):
            signal(((row + d) % 16, 2 * x + cc))
    signal(sibling)
    for d in range(1, 4):
        for cc in range(2):
            signal((row, 2 * ((x + d) % 4) + cc))
    pl.semaphore_wait(barrier, 37)

    def b1_copy(d):
        target = (col + d) % 8
        return pltpu.make_async_remote_copy(
            src_ref=integ.at[:, target], dst_ref=recv_b.at[col],
            send_sem=b1_send, recv_sem=b1_recv,
            device_id=(row, target), device_id_type=MESH,
        )

    for d in range(1, 8):
        b1_copy(d).start()
    pltpu.make_async_copy(integ.at[:, col], recv_b.at[col], b1_recv).start()

    def a1_copy(d, cc):
        target = (row + d) % 16
        return pltpu.make_async_remote_copy(
            src_ref=amp.at[target, pl.ds(2 * cc, 2)], dst_ref=recv_a.at[core * 16 + row],
            send_sem=a1_send, recv_sem=a1_recv,
            device_id=(target, 2 * x + cc), device_id_type=MESH,
        )

    for d in range(1, 16):
        for cc in range(2):
            a1_copy(d, cc).start()
    a1_copy(0, 1 - core).start()
    pltpu.make_async_copy(amp.at[row, pl.ds(2 * core, 2)], recv_a.at[core * 16 + row], a1_recv).start()

    for g in range(4):
        grp_a[g][:, cap2] = jnp.zeros((2, TILE, 128), jnp.bfloat16)
        grp_b[g][cap2] = jnp.zeros((2, TILE, 128), jnp.bfloat16)
    half = lax.broadcasted_iota(jnp.int32, (TILE, 128), 1) // TILE

    def mixed(first, second, parity):
        turned = pltpu.roll(second.astype(jnp.float32), TILE, 1)
        return jnp.where(half == parity, first.astype(jnp.float32), turned).astype(jnp.bfloat16)

    def ring(which, buf, pos, cap, target_of):
        right, left = (pos + 1) % 4, (pos + 3) % 4
        cut = cap // 2

        def copy(src, dst, to, k, s, e):
            return pltpu.make_async_remote_copy(
                src_ref=buf(src, s, e), dst_ref=buf(dst, s, e), send_sem=ring_send.at[which, k],
                recv_sem=ring_recv.at[which, k], device_id=target_of(to), device_id_type=MESH,
            )

        return (copy(0, 3, right, 0, 0, cap), copy(0, 1, left, 1, 0, cap),
                copy(3, 2, right, 2, 0, cut), copy(1, 2, left, 3, cut, cap))

    def part(ref, s, e):
        return ref.at[pl.ds(s, e - s)]

    def ring_b1_copies():
        right, left, opp = (p + 1) % 4, (p + 3) % 4, (p + 2) % 4
        cut = cap1 // 2

        def copy(block, to, k, s, e):
            ref = grp_b1.at[block, pl.ds(s, e - s)]
            return pltpu.make_async_remote_copy(
                src_ref=ref, dst_ref=ref, send_sem=ring_send.at[0, k], recv_sem=ring_recv.at[0, k],
                device_id=(row_of(to, q), col), device_id_type=MESH,
            )

        return (copy(p, right, 0, 0, cap1), copy(p, left, 1, 0, cap1),
                copy(left, right, 2, 0, cut), copy(right, left, 3, cut, cap1))

    ring_b1 = ring_b1_copies()
    ring_b2 = ring(1, lambda g, s, e: part(grp_b[g], s, e), q, cap2, lambda to: (row_of(p, to), col))
    ring_a = ring(2, lambda g, s, e: grp_a[g].at[core, pl.ds(s, e - s)], x, cap2,
                  lambda to: (row, 2 * to + core))

    def sib_copy(g):
        ref = grp_a[g].at[core, pl.ds(0, cap2)]
        return pltpu.make_async_remote_copy(
            src_ref=ref, dst_ref=ref, send_sem=sib_send.at[g], recv_sem=sib_recv.at[g],
            device_id=sibling, device_id_type=MESH,
        )

    def sib_arrival(g):
        there = grp_a[g].at[1 - core, pl.ds(0, cap2)]
        return pltpu.make_async_copy(there, there, sib_recv.at[g])

    pltpu.make_async_copy(recv_b, recv_b, b1_recv).wait()

    def pack_b(s, _):
        e = tab[64 + s]
        for kp in range(2):
            grp_b1[p, s, kp] = mixed(recv_b[e // 2, 2 * kp], recv_b[e // 2, 2 * kp + 1], e % 2)
        return 0

    lax.fori_loop(0, cap1, pack_b, 0)
    ring_b1[0].start()
    ring_b1[1].start()

    pltpu.make_async_copy(recv_a, recv_a, a1_recv).wait()

    def pack_a(s, _):
        e = tab[s]
        grp_a[0][core, s] = mixed(recv_a[e // 2, 0], recv_a[e // 2, 1], e % 2)
        return 0

    lax.fori_loop(0, cap2, pack_a, 0)
    ring_a[0].start()
    ring_a[1].start()
    sib_copy(0).start()

    ring_b1[0].wait_recv()
    ring_b1[2].start()
    ring_b1[1].wait_recv()
    ring_b1[3].start()
    ring_b1[2].wait_recv()
    ring_b1[3].wait_recv()

    def pack_b2(s, _):
        e = tab[128 + s]
        grp_b[0][s] = grp_b1[e // 16, e % 16]
        return 0

    lax.fori_loop(0, cap2, pack_b2, 0)
    ring_b2[0].start()
    ring_b2[1].start()

    def expand_a(rel):
        g = (x + rel) % 4

        def body(a, _):
            for cc in range(4):
                slot = jnp.minimum(tab[192 + g * 64 + a * 4 + cc], cap2)
                for kp in range(2):
                    dense_a[g, pl.ds(a * TILE, TILE), pl.ds((2 * cc + kp) * 128, 128)] = grp_a[rel][kp, slot]
            return 0

        lax.fori_loop(0, 16, body, 0)

    def expand_b(rel):
        g = (q + rel) % 4

        def body(pp, _):
            for c in range(16):
                slot = jnp.minimum(tab[448 + g * 64 + pp * 16 + c], cap2)
                for kp in range(2):
                    dense_b[g, c // 4, pl.ds(pp * TILE, TILE), pl.ds(((c % 4) * 2 + kp) * 128, 128)] = (
                        grp_b[rel][slot, kp]
                    )
            return 0

        lax.fori_loop(0, 4, body, 0)

    def product(rel_a, rel_b, first):
        ga, gb = (x + rel_a) % 4, (q + rel_b) % 4

        def body(m, _):
            rows = pl.ds(m * 256, 256)
            part_sum = lax.dot_general(
                dense_a[ga, rows], dense_b[gb, ga], (((1,), (1,)), ((), ())),
                preferred_element_type=jnp.float32,
            )
            if first:
                acc[gb, rows] = part_sum
            else:
                acc[gb, rows] += part_sum
            return 0

        lax.fori_loop(0, 4, body, 0)

    ring_a[0].wait_recv()
    ring_a[2].start()
    sib_copy(3).start()
    ring_a[1].wait_recv()
    ring_a[3].start()
    sib_copy(1).start()

    expand_b(0)
    sib_arrival(0).wait()
    expand_a(0)
    product(0, 0, True)

    ring_a[2].wait_recv()
    ring_a[3].wait_recv()
    sib_copy(2).start()

    ring_b2[0].wait_recv()
    ring_b2[2].start()
    ring_b2[1].wait_recv()
    ring_b2[3].start()

    for rel in (3, 1, 2):
        sib_arrival(rel).wait()
        expand_a(rel)
        product(rel, 0, False)

    def finish(rel_b):
        expand_b(rel_b)
        for rel in (0, 3, 1, 2):
            product(rel, rel_b, rel == 0)

    finish(3)
    finish(1)
    ring_b2[2].wait_recv()
    ring_b2[3].wait_recv()
    finish(2)

    def narrow(t, _):
        rows = pl.ds((t % 8) * 128, 128)
        out[t // 8, rows] = acc[t // 8, rows].astype(jnp.bfloat16)
        return 0

    lax.fori_loop(0, 32, narrow, 0)

    for d in range(1, 8):
        b1_copy(d).wait_send()
    for d in range(1, 16):
        for cc in range(2):
            a1_copy(d, cc).wait_send()
    a1_copy(0, 1 - core).wait_send()
    for r in (ring_b1, ring_b2, ring_a):
        for c in r:
            c.wait_send()
    for g in range(4):
        sib_copy(g).wait_send()


def contract(level, tab, amp, integ):
    cap1, cap2 = LEVELS[level]
    bf16 = jnp.bfloat16
    dma = pltpu.SemaphoreType.DMA
    return pl.pallas_call(
        functools.partial(comm_kernel, cap1, cap2),
        out_shape=jax.ShapeDtypeStruct((4, 1024, 256), bf16),
        in_specs=[
            pl.BlockSpec(memory_space=pltpu.SMEM),
            pl.BlockSpec(memory_space=pl.ANY),
            pl.BlockSpec(memory_space=pl.ANY),
        ],
        out_specs=pl.BlockSpec(memory_space=pltpu.VMEM),
        scratch_shapes=[
            pltpu.VMEM((32, 2, TILE, 128), bf16),
            pltpu.VMEM((8, 4, TILE, 128), bf16),
            pltpu.VMEM((4, cap1, 2, TILE, 128), bf16),
            *[pltpu.VMEM((2, cap2 + 1, TILE, 128), bf16)] * 4,
            *[pltpu.VMEM((cap2 + 1, 2, TILE, 128), bf16)] * 4,
            pltpu.VMEM((4, 1024, 1024), bf16),
            pltpu.VMEM((4, 4, 256, 1024), bf16),
            pltpu.VMEM((4, 1024, 256), jnp.float32),
            dma, dma, dma, dma,
            dma((3, 4)), dma((3, 4)), dma((4,)), dma((4,)),
        ],
        compiler_params=pltpu.CompilerParams(
            collective_id=level + 1, has_side_effects=True, vmem_limit_bytes=60 << 20
        ),
    )(tab, amp, integ)


def tables(mask_amp, mask_int):
    row = lax.axis_index("row")
    col = lax.axis_index("col")
    x = col // 2
    core = col % 2

    def rank(m):
        n = m.shape[-1]
        before = jnp.arange(n)[:, None] < jnp.arange(n)[None, :]
        return jnp.sum(m[..., :, None] * before.astype(jnp.int32), axis=-2)

    def listed(m, ranks, code, n):
        hit = (ranks[:, None] == jnp.arange(n)[None, :]) & (m[:, None] > 0)
        return jnp.sum(jnp.where(hit, code[:, None], 0), axis=0)

    m_a = mask_amp.reshape(16, 4, 4).transpose(1, 0, 2).reshape(4, 64)
    rank_a = rank(m_a)
    t = jnp.arange(64)
    a, cc = t // 4, t % 4
    code_a = ((cc // 2) * 16 + a) * 2 + cc % 2
    pick = lambda v, g: lax.dynamic_index_in_dim(v, g, 0, keepdims=False)
    list_a = listed(pick(m_a, x), pick(rank_a, x), code_a, 64)
    slot_a = jnp.where(m_a > 0, rank_a, 64)

    rank_row = rank(mask_int)
    list_b1 = listed(pick(mask_int, row), pick(rank_row, row), jnp.arange(16), 64)

    by_z = mask_int.reshape(4, 4, 16)
    by_y = by_z.transpose(1, 0, 2)
    rk_z = rank_row.reshape(4, 4, 16)
    rk_y = rk_z.transpose(1, 0, 2)
    m_b = jnp.where(core == 0, by_z, by_y).reshape(4, 64)
    rk = jnp.where(core == 0, rk_z, rk_y).reshape(4, 64)
    q = jnp.where(core == 0, row // 4, row % 4)
    rank_b = rank(m_b)
    list_b2 = listed(pick(m_b, q), pick(rank_b, q), (t // 16) * 16 + pick(rk, q), 64)
    slot_b = jnp.where(m_b > 0, rank_b, 64)

    most1 = jnp.max(jnp.sum(mask_int, axis=1))
    most2 = jnp.maximum(
        jnp.max(jnp.sum(m_a, axis=1)),
        jnp.maximum(jnp.max(jnp.sum(by_z, axis=(1, 2))), jnp.max(jnp.sum(by_y, axis=(1, 2)))),
    )
    level = sum(((most1 > c1) | (most2 > c2)).astype(jnp.int32) for c1, c2 in LEVELS[:-1])
    tab = jnp.concatenate([list_a, list_b1, list_b2, slot_a.reshape(-1), slot_b.reshape(-1)])
    return tab, level


def per_device(
    amplitudes, cycle_integrals, mask_amp, mask_int, occupied_i, occupied_j, virtual_energy
):
    tab, level = tables(mask_amp, mask_int)
    branches = [functools.partial(contract, k) for k in range(len(LEVELS))]
    cycle = lax.switch(level, branches, tab, amplitudes, cycle_integrals)
    core = lax.axis_index("col") % 2
    blocks = cycle.reshape(4, 1024, 4, TILE)
    cycle = jnp.where(core == 0, blocks.transpose(1, 0, 2, 3), blocks.transpose(1, 2, 0, 3)).reshape(1024, 1024)
    denominator = virtual_energy[:, None] + virtual_energy[None, :] - occupied_i[0] - occupied_j[0]
    result = cycle.astype(jnp.float32) / denominator
    return result.astype(jnp.bfloat16)[None, None]


def solution(mesh):
    in_specs = (
        P(None, None, "row", "col"),
        P(None, None, "row", "col"),
        P(),
        P(),
        P("row"),
        P("col"),
        P(),
    )
    out_specs = P("row", "col", None, None)
    return jax.shard_map(
        per_device, mesh=mesh, in_specs=in_specs, out_specs=out_specs, check_vma=False
    )
```

```python
import functools

import jax
import jax.numpy as jnp
from jax import lax
from jax.experimental import pallas as pl
from jax.experimental.pallas import tpu as pltpu
from jax.sharding import PartitionSpec as P

TILE = 64
MESH = pl.DeviceIdType.MESH

LEVELS = ((9, 24, 24), (9, 26, 26), (10, 28, 28), (12, 34, 34), (16, 64, 64))


def place():
    row = lax.axis_index("row")
    col = lax.axis_index("col")
    core = col % 2
    z, y = row // 4, row % 4
    p = (1 - core) * y + core * z
    q = (1 - core) * z + core * y
    return row, col, col // 2, core, p, q


def row_at(core, p, q):
    return (p * 4 + q) * core + (q * 4 + p) * (1 - core)


def ring_places(here):
    away = [(g - here + 4) % 4 for g in range(4)]
    return [2 * (d == 1) + 3 * (d == 2) + 1 * (d == 3) for d in away]


def table_kernel(mask_a, mask_b, tab, level):
    row, col, x, core, p, q = place()

    def clear(t, _):
        for k in range(16):
            tab[t * 16 + k] = 0
        return 0

    lax.fori_loop(0, 12, clear, 0)

    def scan_a(a, carry):
        count, totals = carry[0], list(carry[1:])
        for cc in range(4):
            tab[count] = ((cc // 2) * 16 + a) * 2 + cc % 2
            count += mask_a[a, 4 * x + cc]
        for g in range(4):
            for cc in range(4):
                totals[g] += mask_a[a, 4 * g + cc]
        return (count, *totals)

    zero = jnp.int32(0)
    most_a = functools.reduce(jnp.maximum, lax.fori_loop(0, 16, scan_a, (zero,) * 5)[1:])

    def scan_row(c, count):
        tab[64 + count] = c
        return count + mask_b[row, c]

    lax.fori_loop(0, 16, scan_row, zero, unroll=True)

    def scan_b(g, carry):
        most_row, most_z, by_y = carry[0], carry[1], list(carry[2:])
        total = zero
        for k in range(4):
            count = zero
            for c in range(16):
                count += mask_b[4 * g + k, c]
            most_row = jnp.maximum(most_row, count)
            by_y[k] += count
            total += count
        return (most_row, jnp.maximum(most_z, total), *by_y)

    most_row, most_z, *by_y = lax.fori_loop(0, 4, scan_b, (zero,) * 6)
    most_b = functools.reduce(jnp.maximum, by_y, most_z)

    def scan_pool(k, count):
        rank = zero
        here = row_at(core, k, q)
        for c in range(16):
            tab[128 + count] = k * 16 + rank
            bit = mask_b[here, c]
            count += bit
            rank += bit
        return count

    lax.fori_loop(0, 4, scan_pool, zero)

    found = zero
    for c1, ca, cb in LEVELS[:-1]:
        found += ((most_row > c1) | (most_a > ca) | (most_b > cb)).astype(jnp.int32)
    level[0] = found


def tables(mask_amp, mask_int):
    smem = pl.BlockSpec(memory_space=pltpu.SMEM)
    return pl.pallas_call(
        table_kernel,
        out_shape=(jax.ShapeDtypeStruct((192,), jnp.int32), jax.ShapeDtypeStruct((1,), jnp.int32)),
        in_specs=[smem, smem],
        out_specs=(smem, smem),
    )(mask_amp, mask_int)


def comm_kernel(
    cap1, capa, capb, tab, mask_a, mask_b, amp, integ, out,
    recv_a, recv_b, grp_b1, ga0, ga1, ga2, ga3, gb0, gb1, gb2, gb3, dense_a, dense_b, acc, narrow,
    a1_send, a1_recv, b1_send, b1_recv, ring_send, ring_recv, sib_send, sib_recv, out_sem,
):
    grp_a, grp_b = (ga0, ga1, ga2, ga3), (gb0, gb1, gb2, gb3)
    row, col, x, core, p, q = place()
    sibling = (row, 2 * x + 1 - core)

    barrier = pltpu.get_barrier_semaphore()

    def signal(target):
        pl.semaphore_signal(barrier, inc=1, device_id=target, device_id_type=MESH)

    for d in range(1, 4):
        for cc in range(2):
            signal((row, 2 * ((x + d) % 4) + cc))
    signal(sibling)
    for d in range(1, 16):
        for cc in range(2):
            signal(((row + d) % 16, 2 * x + cc))
    pl.semaphore_wait(barrier, 37)

    def b1_copy(d):
        target = (col + d) % 8
        return pltpu.make_async_remote_copy(
            src_ref=integ.at[:, target], dst_ref=recv_b.at[col],
            send_sem=b1_send, recv_sem=b1_recv,
            device_id=(row, target), device_id_type=MESH,
        )

    for d in range(1, 8):
        b1_copy(d).start()
    pltpu.make_async_copy(integ.at[:, col], recv_b.at[col], b1_recv).start()

    def a1_copy(d, cc):
        target = (row + d) % 16
        return pltpu.make_async_remote_copy(
            src_ref=amp.at[target, pl.ds(2 * cc, 2)], dst_ref=recv_a.at[core * 16 + row],
            send_sem=a1_send, recv_sem=a1_recv,
            device_id=(target, 2 * x + cc), device_id_type=MESH,
        )

    for d in range(1, 16):
        for cc in range(2):
            a1_copy(d, cc).start()
    a1_copy(0, 1 - core).start()
    pltpu.make_async_copy(amp.at[row, pl.ds(2 * core, 2)], recv_a.at[core * 16 + row], a1_recv).start()

    for g in range(4):
        grp_a[g][:, capa] = jnp.zeros((2, TILE, 128), jnp.bfloat16)
        grp_b[g][capb] = jnp.zeros((2, TILE, 128), jnp.bfloat16)
    half = lax.broadcasted_iota(jnp.int32, (TILE, 128), 1) // TILE

    def mixed(first, second, parity):
        turned = pltpu.roll(second.astype(jnp.float32), TILE, 1)
        return jnp.where(half == parity, first.astype(jnp.float32), turned).astype(jnp.bfloat16)

    class Ring:
        def __init__(self, which, view, pos, cap, target_of, absolute=False):
            right, left, cut = (pos + 1) % 4, (pos + 3) % 4, cap // 2

            def copy(k, src, dst, to, s, e):
                if absolute:
                    src = dst = (pos + src) % 4
                return pltpu.make_async_remote_copy(
                    src_ref=view(src, s, e), dst_ref=view(dst, s, e), send_sem=ring_send.at[which, k],
                    recv_sem=ring_recv.at[which, k], device_id=target_of(to), device_id_type=MESH,
                )

            self.first_right = copy(0, 0, 3, right, 0, cut)
            self.first_left = copy(1, 0, 1, left, cut, cap)
            self.rest_right = copy(2, 0, 3, right, cut, cap)
            self.rest_left = copy(3, 0, 1, left, 0, cut)
            self.on_right = copy(4, 3, 2, right, 0, cut)
            self.on_left = copy(5, 1, 2, left, cut, cap)

        def start(self):
            self.first_right.start()
            self.first_left.start()
            self.rest_right.start()
            self.rest_left.start()

        def forward(self):
            self.first_right.wait_recv()
            self.on_right.start()
            self.first_left.wait_recv()
            self.on_left.start()

        def wait_opposite(self):
            self.on_right.wait_recv()
            self.on_left.wait_recv()

        def wait_sends(self):
            for c in (self.first_right, self.first_left, self.rest_right, self.rest_left,
                      self.on_right, self.on_left):
                c.wait_send()

    ring_b1 = Ring(0, lambda at, s, e: grp_b1.at[at, pl.ds(s, e - s)], p, cap1,
                   lambda to: (row_at(core, to, q), col), absolute=True)
    ring_b2 = Ring(1, lambda g, s, e: grp_b[g].at[pl.ds(s, e - s)], q, capb,
                   lambda to: (row_at(core, p, to), col))
    ring_a = Ring(2, lambda g, s, e: grp_a[g].at[core, pl.ds(s, e - s)], x, capa,
                  lambda to: (row, 2 * to + core))

    def sib_copy(g):
        ref = grp_a[g].at[core, pl.ds(0, capa)]
        return pltpu.make_async_remote_copy(
            src_ref=ref, dst_ref=ref, send_sem=sib_send.at[g], recv_sem=sib_recv.at[g],
            device_id=sibling, device_id_type=MESH,
        )

    def sib_wait(g):
        there = grp_a[g].at[1 - core, pl.ds(0, capa)]
        pltpu.make_async_copy(there, there, sib_recv.at[g]).wait()

    def expand_a(rel, pos):
        g = (x + rel) % 4

        def body(a, count):
            for cc in range(4):
                bit = mask_a[a, 4 * g + cc]
                slot = jnp.where(bit > 0, count, capa)
                count += bit
                for kp in range(2):
                    dense_a[pl.ds(a * TILE, TILE), pl.ds(pos * 1024 + (2 * cc + kp) * 128, 128)] = (
                        grp_a[rel][kp, slot]
                    )
            return count

        lax.fori_loop(0, 16, body, jnp.int32(0))

    def expand_b(rel, pos):
        g = (q + rel) % 4
        first = [pl.multiple_of(1024 * v, 1024) for v in ring_places(x)]

        def body(k, count):
            here = row_at(core, k, g)
            for c in range(16):
                bit = mask_b[here, c]
                slot = jnp.where(bit > 0, count, capb)
                count += bit
                for kp in range(2):
                    lanes = pl.ds(first[c // 4] + (2 * (c % 4) + kp) * 128, 128)
                    dense_b[pl.ds(pos * 256 + k * TILE, TILE), lanes] = grp_b[rel][slot, kp]
            return count

        lax.fori_loop(0, 4, body, jnp.int32(0))

    def by_rows(done, columns, depth):
        def body(t, _):
            rows = pl.ds(t * 512, 512)
            done(rows, lax.dot_general(
                dense_a[rows, pl.ds(*depth)], dense_b[pl.ds(*columns), pl.ds(*depth)],
                (((1,), (1,)), ((), ())), preferred_element_type=jnp.float32,
            ))
            return 0

        lax.fori_loop(0, 2, body, 0)

    def out_copy(rel, pos):
        return pltpu.make_async_copy(narrow.at[pos], out.at[(q + rel) % 4], out_sem.at[pos])

    pltpu.make_async_copy(recv_b, recv_b, b1_recv).wait()

    def pack_b(s, _):
        e = tab[64 + s]
        for kp in range(2):
            grp_b1[p, s, kp] = mixed(recv_b[e // 2, 2 * kp], recv_b[e // 2, 2 * kp + 1], e % 2)
        return 0

    lax.fori_loop(0, cap1, pack_b, 0)
    ring_b1.start()
    ring_b1.forward()

    pltpu.make_async_copy(recv_a, recv_a, a1_recv).wait()

    def pack_a(s, _):
        e = tab[s]
        grp_a[0][core, s] = mixed(recv_a[e // 2, 0], recv_a[e // 2, 1], e % 2)
        return 0

    lax.fori_loop(0, capa, pack_a, 0)
    ring_a.start()
    sib_copy(0).start()

    ring_b1.rest_right.wait_recv()
    ring_b1.rest_left.wait_recv()
    ring_b1.wait_opposite()

    def pack_b2(s, _):
        e = tab[128 + s]
        grp_b[0][s] = grp_b1[e // 16, e % 16]
        return 0

    lax.fori_loop(0, capb, pack_b2, 0)
    ring_b2.start()

    ring_a.forward()
    expand_b(0, 0)
    sib_wait(0)
    expand_a(0, 0)

    def put_own(rows, value):
        acc[rows, 0:256] = value

    by_rows(put_own, (0, 256), (0, 1024))

    ring_b2.forward()
    ring_a.rest_right.wait_recv()
    sib_copy(3).start()
    ring_a.rest_left.wait_recv()
    sib_copy(1).start()
    sib_wait(3)
    expand_a(3, 1)
    sib_wait(1)
    expand_a(1, 2)

    def add_own(rows, value):
        acc[rows, 0:256] += value

    by_rows(add_own, (0, 256), (1024, 2048))

    ring_b2.rest_right.wait_recv()
    expand_b(3, 1)
    ring_b2.rest_left.wait_recv()
    expand_b(1, 2)

    def put_sides(rows, value):
        acc[rows, 256:768] = value

    by_rows(put_sides, (256, 512), (0, 3072))

    ring_a.wait_opposite()
    sib_copy(2).start()
    sib_wait(2)
    expand_a(2, 3)

    def finish_three(rows, value):
        total = (acc[rows] + value).astype(jnp.bfloat16)
        for g in range(3):
            narrow[g, rows] = total[:, g * 256:(g + 1) * 256]

    by_rows(finish_three, (0, 768), (3072, 1024))
    for pos, rel in enumerate((0, 3, 1)):
        out_copy(rel, pos).start()

    ring_b2.wait_opposite()
    expand_b(2, 3)

    def finish_last(rows, value):
        narrow[3, rows] = value.astype(jnp.bfloat16)

    by_rows(finish_last, (768, 256), (0, 4096))
    out_copy(2, 3).start()

    for d in range(1, 8):
        b1_copy(d).wait_send()
    for d in range(1, 16):
        for cc in range(2):
            a1_copy(d, cc).wait_send()
    a1_copy(0, 1 - core).wait_send()
    for ring in (ring_b1, ring_b2, ring_a):
        ring.wait_sends()
    for g in range(4):
        sib_copy(g).wait_send()
    for pos, rel in enumerate((0, 3, 1, 2)):
        out_copy(rel, pos).wait()


def contract(level, tab, mask_amp, mask_int, amp, integ):
    cap1, capa, capb = LEVELS[level]
    bf16 = jnp.bfloat16
    dma = pltpu.SemaphoreType.DMA
    smem = pl.BlockSpec(memory_space=pltpu.SMEM)
    anywhere = pl.BlockSpec(memory_space=pl.ANY)
    return pl.pallas_call(
        functools.partial(comm_kernel, cap1, capa, capb),
        out_shape=jax.ShapeDtypeStruct((4, 1024, 256), bf16),
        in_specs=[smem, smem, smem, anywhere, anywhere],
        out_specs=anywhere,
        scratch_shapes=[
            pltpu.VMEM((32, 2, TILE, 128), bf16),
            pltpu.VMEM((8, 4, TILE, 128), bf16),
            pltpu.VMEM((4, cap1, 2, TILE, 128), bf16),
            *[pltpu.VMEM((2, capa + 1, TILE, 128), bf16)] * 4,
            *[pltpu.VMEM((capb + 1, 2, TILE, 128), bf16)] * 4,
            pltpu.VMEM((1024, 4096), bf16),
            pltpu.VMEM((1024, 4096), bf16),
            pltpu.VMEM((1024, 768), jnp.float32),
            pltpu.VMEM((4, 1024, 256), bf16),
            dma, dma, dma, dma,
            dma((3, 6)), dma((3, 6)), dma((4,)), dma((4,)), dma((4,)),
        ],
        compiler_params=pltpu.CompilerParams(
            collective_id=level + 1, has_side_effects=True, vmem_limit_bytes=60 << 20
        ),
    )(tab, mask_amp, mask_int, amp, integ)


def update_kernel(cycle, energy_a, energy_b, occ_i, occ_j, out):
    core = lax.axis_index("col") % 2
    rows = out.shape[2]
    down = jnp.transpose(jnp.broadcast_to(energy_a[...], (128, rows)))

    def emit(m, value):
        lanes = pl.ds(m * 128, 128)
        denominator = down + energy_b[:, lanes] - occ_i[0] - occ_j[0]
        out[0, 0, :, lanes] = (value.astype(jnp.float32) / denominator).astype(jnp.bfloat16)

    @pl.when(core == 0)
    def _():
        for m in range(8):
            emit(m, cycle[m // 2, :, pl.ds((m % 2) * 128, 128)])

    @pl.when(core == 1)
    def _():
        for m in range(8):
            k, g = m // 2, 2 * (m % 2)
            pair = [cycle[g + s, :, pl.ds((k // 2) * 128, 128)].astype(jnp.float32)
                    [:, (k % 2) * TILE:(k % 2 + 1) * TILE] for s in range(2)]
            emit(m, jnp.concatenate(pair, axis=1))


def update(cycle, virtual_energy, occupied_i, occupied_j):
    energies = virtual_energy.reshape(1, 1024)
    smem = pl.BlockSpec(memory_space=pltpu.SMEM)
    rows = 128
    return pl.pallas_call(
        update_kernel,
        grid=(1024 // rows,),
        out_shape=jax.ShapeDtypeStruct((1, 1, 1024, 1024), jnp.bfloat16),
        in_specs=[
            pl.BlockSpec((4, rows, 256), lambda t: (0, t, 0)),
            pl.BlockSpec((1, rows), lambda t: (0, t)),
            pl.BlockSpec((1, 1024), lambda t: (0, 0)),
            smem, smem,
        ],
        out_specs=pl.BlockSpec((1, 1, rows, 1024), lambda t: (0, 0, t, 0)),
    )(cycle, energies, energies, occupied_i, occupied_j)


def per_device(
    amplitudes, cycle_integrals, mask_amp, mask_int, occupied_i, occupied_j, virtual_energy
):
    tab, level = tables(mask_amp, mask_int)
    branches = [functools.partial(contract, k) for k in range(len(LEVELS))]
    cycle = lax.switch(level[0], branches, tab, mask_amp, mask_int, amplitudes, cycle_integrals)
    return update(cycle, virtual_energy, occupied_i, occupied_j)


def solution(mesh):
    in_specs = (
        P(None, None, "row", "col"),
        P(None, None, "row", "col"),
        P(),
        P(),
        P("row"),
        P("col"),
        P(),
    )
    out_specs = P("row", "col", None, None)
    return jax.shard_map(
        per_device, mesh=mesh, in_specs=in_specs, out_specs=out_specs, check_vma=False
    )
```

```python
import functools

import jax
import jax.numpy as jnp
from jax import lax
from jax.experimental import pallas as pl
from jax.experimental.pallas import tpu as pltpu
from jax.sharding import PartitionSpec as P

TILE = 64
HALF = 32
MESH = pl.DeviceIdType.MESH

LEVELS = ((9, 24, 24), (10, 28, 28), (12, 34, 34), (16, 64, 64))


def place():
    row = lax.axis_index("row")
    col = lax.axis_index("col")
    core = col % 2
    z, y = row // 4, row % 4
    p = (1 - core) * y + core * z
    q = (1 - core) * z + core * y
    return row, col, col // 2, core, p, q


def row_at(core, p, q):
    return (p * 4 + q) * core + (q * 4 + p) * (1 - core)


def ring_places(here):
    away = [(g - here + 4) % 4 for g in range(4)]
    return [2 * (d == 1) + 3 * (d == 2) + 1 * (d == 3) for d in away]


def table_kernel(mask_a, mask_b, tab, level):
    row, col, x, core, p, q = place()

    def clear(t, _):
        for k in range(16):
            tab[t * 16 + k] = 0
        return 0

    lax.fori_loop(0, 12, clear, 0)

    def scan_a(a, carry):
        count, totals = carry[0], list(carry[1:])
        for cc in range(4):
            tab[count] = ((cc // 2) * 16 + a) * 2 + cc % 2
            count += mask_a[a, 4 * x + cc]
        for g in range(4):
            for cc in range(4):
                totals[g] += mask_a[a, 4 * g + cc]
        return (count, *totals)

    zero = jnp.int32(0)
    most_a = functools.reduce(jnp.maximum, lax.fori_loop(0, 16, scan_a, (zero,) * 5)[1:])

    def scan_row(c, count):
        tab[64 + count] = c
        return count + mask_b[row, c]

    lax.fori_loop(0, 16, scan_row, zero, unroll=True)

    def scan_b(g, carry):
        most_row, most_z, by_y = carry[0], carry[1], list(carry[2:])
        total = zero
        for k in range(4):
            count = zero
            for c in range(16):
                count += mask_b[4 * g + k, c]
            most_row = jnp.maximum(most_row, count)
            by_y[k] += count
            total += count
        return (most_row, jnp.maximum(most_z, total), *by_y)

    most_row, most_z, *by_y = lax.fori_loop(0, 4, scan_b, (zero,) * 6)
    most_b = functools.reduce(jnp.maximum, by_y, most_z)

    def scan_pool(k, count):
        rank = zero
        here = row_at(core, k, q)
        for c in range(16):
            tab[128 + count] = k * 16 + rank
            bit = mask_b[here, c]
            count += bit
            rank += bit
        return count

    lax.fori_loop(0, 4, scan_pool, zero)

    found = zero
    for c1, ca, cb in LEVELS[:-1]:
        found += ((most_row > c1) | (most_a > ca) | (most_b > cb)).astype(jnp.int32)
    level[0] = found


def tables(mask_amp, mask_int):
    smem = pl.BlockSpec(memory_space=pltpu.SMEM)
    return pl.pallas_call(
        table_kernel,
        out_shape=(jax.ShapeDtypeStruct((192,), jnp.int32), jax.ShapeDtypeStruct((1,), jnp.int32)),
        in_specs=[smem, smem],
        out_specs=(smem, smem),
    )(mask_amp, mask_int)


def comm_kernel(
    cap1, capa, capb, tab_in, mask_a_in, mask_b_in, occ_i_in, occ_j_in, energy_in, amp, integ, out,
    tab, mask_a, mask_b, occ_i, occ_j, energy,
    ra0, ra1, rb0, rb1, b10, b11, ga0, ga1, ga2, ga3, gb0, gb1, gb2, gb3, gb4, gb5, gb6, gb7,
    dense_a, dense_b, acc, narrow, inverse, staged, small_sem,
    a1_send, a1_recv, b1_send, b1_recv, ring_send, ring_recv, sib_send, sib_recv, out_sem,
):
    recv_a, recv_b, grp_b1 = (ra0, ra1), (rb0, rb1), (b10, b11)
    grp_a, grp_b = (ga0, ga1, ga2, ga3), ((gb0, gb1), (gb2, gb3), (gb4, gb5), (gb6, gb7))
    row, col, x, core, p, q = place()
    sibling = (row, 2 * x + 1 - core)

    barrier = pltpu.get_barrier_semaphore()

    def signal(target):
        pl.semaphore_signal(barrier, inc=1, device_id=target, device_id_type=MESH)

    for d in range(1, 16):
        for cc in range(2):
            signal(((row + d) % 16, 2 * x + cc))
    for d in range(1, 4):
        for cc in range(2):
            signal((row, 2 * ((x + d) % 4) + cc))
    signal(sibling)
    small = [
        pltpu.make_async_copy(src, dst, small_sem.at[n]) for n, (src, dst) in enumerate((
            (tab_in, tab), (mask_a_in, mask_a), (mask_b_in, mask_b),
            (occ_i_in, occ_i), (occ_j_in, occ_j), (energy_in, energy),
        ))
    ]
    for copy in small:
        copy.start()
    pl.semaphore_wait(barrier, 37)

    def b1_copy(d, h):
        target = (col + d) % 8
        return pltpu.make_async_remote_copy(
            src_ref=integ.at[pl.ds(2 * h, 2), target], dst_ref=recv_b[h].at[col],
            send_sem=b1_send.at[h], recv_sem=b1_recv.at[h],
            device_id=(row, target), device_id_type=MESH,
        )

    def a1_copy(d, cc, h):
        target = (row + d) % 16
        return pltpu.make_async_remote_copy(
            src_ref=amp.at[target, pl.ds(2 * cc, 2), pl.ds(h * HALF, HALF)],
            dst_ref=recv_a[h].at[core * 16 + row],
            send_sem=a1_send.at[h], recv_sem=a1_recv.at[h],
            device_id=(target, 2 * x + cc), device_id_type=MESH,
        )

    a1_targets = [(d, cc) for d in range(1, 16) for cc in range(2)]
    for h in range(2):
        for d in range(1, 8):
            b1_copy(d, h).start()
        pltpu.make_async_copy(
            integ.at[pl.ds(2 * h, 2), col], recv_b[h].at[col], b1_recv.at[h]
        ).start()
        for d, cc in a1_targets:
            a1_copy(d, cc, h).start()
        a1_copy(0, 1 - core, h).start()
        pltpu.make_async_copy(
            amp.at[row, pl.ds(2 * core, 2), pl.ds(h * HALF, HALF)],
            recv_a[h].at[core * 16 + row], a1_recv.at[h],
        ).start()

    for g in range(4):
        grp_a[g][:, :, capa] = jnp.zeros((2, 2, HALF, 128), jnp.bfloat16)
        for h in range(2):
            grp_b[g][h][capb] = jnp.zeros((TILE, 128), jnp.bfloat16)

    def mixed(first, second, parity):
        side = lax.broadcasted_iota(jnp.int32, first.shape, 1) // TILE
        turned = pltpu.roll(second.astype(jnp.float32), TILE, 1)
        return jnp.where(side == parity, first.astype(jnp.float32), turned).astype(jnp.bfloat16)

    class Ring:
        def __init__(self, which, view, pos, cap, target_of, absolute=False):
            right, left, cut = (pos + 1) % 4, (pos + 3) % 4, cap // 2

            def copy(h, k, src, dst, to, s, e):
                if absolute:
                    src = dst = (pos + src) % 4
                return pltpu.make_async_remote_copy(
                    src_ref=view(h, src, s, e), dst_ref=view(h, dst, s, e),
                    send_sem=ring_send.at[which, h, k], recv_sem=ring_recv.at[which, h, k],
                    device_id=target_of(to), device_id_type=MESH,
                )

            self.copies = [(
                copy(h, 0, 0, 3, right, 0, cap), copy(h, 1, 0, 1, left, 0, cap),
                copy(h, 2, 3, 2, right, 0, cut), copy(h, 3, 1, 2, left, cut, cap),
            ) for h in range(2)]

        def start(self, h):
            self.copies[h][0].start()
            self.copies[h][1].start()

        def forward(self, h):
            for k in range(2):
                self.copies[h][k].wait_recv()
                self.copies[h][2 + k].start()

        def wait_opposite(self, h):
            self.copies[h][2].wait_recv()
            self.copies[h][3].wait_recv()

        def wait_sends(self):
            for h in range(2):
                for c in self.copies[h]:
                    c.wait_send()

    ring_b1 = Ring(0, lambda h, at, s, e: grp_b1[h].at[at, pl.ds(s, e - s)], p, cap1,
                   lambda to: (row_at(core, to, q), col), absolute=True)
    ring_b2 = Ring(1, lambda h, g, s, e: grp_b[g][h].at[pl.ds(s, e - s)], q, capb,
                   lambda to: (row_at(core, p, to), col))
    ring_a = Ring(2, lambda h, g, s, e: grp_a[g].at[core, h, pl.ds(s, e - s)], x, capa,
                  lambda to: (row, 2 * to + core))

    def sib_copy(g, h):
        ref = grp_a[g].at[core, h, pl.ds(0, capa)]
        return pltpu.make_async_remote_copy(
            src_ref=ref, dst_ref=ref, send_sem=sib_send.at[g, h], recv_sem=sib_recv.at[g, h],
            device_id=sibling, device_id_type=MESH,
        )

    def sib_wait(g):
        for h in range(2):
            there = grp_a[g].at[1 - core, h, pl.ds(0, capa)]
            pltpu.make_async_copy(there, there, sib_recv.at[g, h]).wait()

    def expand_a(rel, pos):
        g = (x + rel) % 4

        def body(a, count):
            for cc in range(4):
                bit = mask_a[a, 4 * g + cc]
                slot = jnp.where(bit > 0, count, capa)
                count += bit
                for kp in range(2):
                    lanes = pl.ds(kp * 2048 + pos * 512 + cc * 128, 128)
                    for h in range(2):
                        dense_a[pl.ds(a * TILE + h * HALF, HALF), lanes] = grp_a[rel][kp, h, slot]
            return count

        lax.fori_loop(0, 16, body, jnp.int32(0))

    def expand_b(rel, pos, kp):
        g = (q + rel) % 4
        first = [pl.multiple_of(512 * v, 512) for v in ring_places(x)]

        def body(k, count):
            here = row_at(core, k, g)
            for c in range(16):
                bit = mask_b[here, c]
                slot = jnp.where(bit > 0, count, capb)
                count += bit
                lanes = pl.ds(kp * 2048 + first[c // 4] + (c % 4) * 128, 128)
                dense_b[pl.ds(pos * 256 + k * TILE, TILE), lanes] = grp_b[rel][kp][slot]
            return count

        lax.fori_loop(0, 4, body, jnp.int32(0))

    def by_rows(done, columns, pairs, places):
        def body(t, _):
            rows = pl.ds(t * 512, 512)
            total = None
            for kp in pairs:
                depth = pl.ds(kp * 2048 + places[0] * 512, places[1] * 512)
                part = lax.dot_general(
                    dense_a[rows, depth], dense_b[pl.ds(*columns), depth],
                    (((1,), (1,)), ((), ())), preferred_element_type=jnp.float32,
                )
                total = part if total is None else total + part
            done(rows, pl.ds(*columns), total)
            return 0

        lax.fori_loop(0, 2, body, 0)

    def put(rows, lanes, value):
        acc[rows, lanes] = value

    def add(rows, lanes, value):
        acc[rows, lanes] += value

    def pack_b(h):
        def body(s, _):
            e = tab[64 + s]
            grp_b1[h][p, s] = mixed(recv_b[h][e // 2, 0], recv_b[h][e // 2, 1], e % 2)
            return 0

        lax.fori_loop(0, cap1, body, 0)

    def pack_a(h):
        def body(s, _):
            e = tab[s]
            grp_a[0][core, h, s] = mixed(recv_a[h][e // 2, 0], recv_a[h][e // 2, 1], e % 2)
            return 0

        lax.fori_loop(0, capa, body, 0)

    def pool_b(h):
        def body(s, _):
            e = tab[128 + s]
            grp_b[0][h][s] = grp_b1[h][e // 16, e % 16]
            return 0

        lax.fori_loop(0, capb, body, 0)

    def invert(t, _):
        rows = pl.ds(t * 128, 128)
        down = jnp.transpose(jnp.broadcast_to(energy[:, rows], (128, 128)))
        for m in range(8):
            lanes = pl.ds(m * 128, 128)
            inverse[rows, lanes] = 1.0 / (down + energy[:, lanes] - occ_i[0] - occ_j[0])
        return 0

    def emit(rows, m, value):
        lanes = pl.ds(pl.multiple_of(m * 128, 128), 128)
        staged[rows, lanes] = (value * inverse[rows, lanes]).astype(jnp.bfloat16)

    def out_copy(m):
        lanes = pl.ds(pl.multiple_of(m * 128, 128), 128)
        return pltpu.make_async_copy(staged.at[:, lanes], out.at[:, lanes], out_sem.at[m])

    def finish_group(g):
        def body(t, _):
            rows = pl.ds(t * 128, 128)
            for s in range(2):
                emit(rows, 2 * g + s, narrow[g, rows, pl.ds(s * 128, 128)].astype(jnp.float32))
            return 0

        lax.fori_loop(0, 8, body, 0)
        for s in range(2):
            out_copy(2 * g + s).start()

    lower = lax.broadcasted_iota(jnp.int32, (128, 128), 1) < TILE

    def finish_pair(h):
        def body(t, _):
            rows = pl.ds(t * 128, 128)
            for k in range(4):
                one, two = [
                    narrow[2 * h + s, rows, pl.ds((k // 2) * 128, 128)].astype(jnp.float32) for s in range(2)
                ]
                if k % 2 == 0:
                    two = pltpu.roll(two, TILE, 1)
                else:
                    one = pltpu.roll(one, TILE, 1)
                emit(rows, 2 * k + h, jnp.where(lower, one, two))
            return 0

        lax.fori_loop(0, 8, body, 0)
        for k in range(4):
            out_copy(2 * k + h).start()

    for copy in small:
        copy.wait()
    lax.fori_loop(0, 8, invert, 0)

    for h in range(2):
        pltpu.make_async_copy(recv_b[h], recv_b[h], b1_recv.at[h]).wait()
        pack_b(h)
        ring_b1.start(h)

    for h in range(2):
        pltpu.make_async_copy(recv_a[h], recv_a[h], a1_recv.at[h]).wait()
        pack_a(h)
        ring_a.start(h)
        sib_copy(0, h).start()
        ring_b1.forward(h)

    for h in range(2):
        ring_b1.wait_opposite(h)
        pool_b(h)
        ring_b2.start(h)
        ring_a.forward(h)
        sib_copy(3, h).start()
        sib_copy(1, h).start()

    for kp in range(2):
        expand_b(0, 0, kp)
    sib_wait(0)
    expand_a(0, 0)
    by_rows(put, (0, 256), (0, 1), (0, 1))

    ring_b2.forward(0)
    sib_wait(3)
    expand_a(3, 1)
    sib_wait(1)
    expand_a(1, 2)
    by_rows(add, (0, 256), (0, 1), (1, 2))
    expand_b(3, 1, 0)
    expand_b(1, 2, 0)
    by_rows(put, (256, 512), (0,), (0, 3))

    ring_b2.forward(1)
    for h in range(2):
        ring_a.wait_opposite(h)
        sib_copy(2, h).start()
    expand_b(3, 1, 1)
    expand_b(1, 2, 1)
    by_rows(add, (256, 512), (1,), (0, 3))

    sib_wait(2)
    expand_a(2, 3)

    def finish_three(rows, lanes, value):
        total = (acc[rows, lanes] + value).astype(jnp.bfloat16)
        for pos, rel in enumerate((0, 3, 1)):
            narrow[(q + rel) % 4, rows] = total[:, pos * 256:(pos + 1) * 256]

    by_rows(finish_three, (0, 768), (0, 1), (3, 1))

    opposite = (q + 2) % 4

    ring_b2.wait_opposite(0)
    expand_b(2, 3, 0)
    by_rows(put, (768, 256), (0,), (0, 4))

    @pl.when(core == 0)
    def _():
        for rel in (0, 3, 1):
            finish_group((q + rel) % 4)

    @pl.when(core == 1)
    def _():
        finish_pair(1 - opposite // 2)

    ring_b2.wait_opposite(1)
    expand_b(2, 3, 1)

    def finish_last(rows, lanes, value):
        narrow[opposite, rows] = (acc[rows, lanes] + value).astype(jnp.bfloat16)

    by_rows(finish_last, (768, 256), (1,), (0, 4))

    @pl.when(core == 0)
    def _():
        finish_group(opposite)

    @pl.when(core == 1)
    def _():
        finish_pair(opposite // 2)

    for h in range(2):
        for d in range(1, 8):
            b1_copy(d, h).wait_send()
        for d, cc in a1_targets:
            a1_copy(d, cc, h).wait_send()
        a1_copy(0, 1 - core, h).wait_send()
        for g in range(4):
            sib_copy(g, h).wait_send()
    for ring in (ring_b1, ring_b2, ring_a):
        ring.wait_sends()
    for m in range(8):
        out_copy(m).wait()


def contract(level, tab, mask_amp, mask_int, occ_i, occ_j, energy, amp, integ):
    cap1, capa, capb = LEVELS[level]
    bf16 = jnp.bfloat16
    dma = pltpu.SemaphoreType.DMA
    anywhere = pl.BlockSpec(memory_space=pl.ANY)
    return pl.pallas_call(
        functools.partial(comm_kernel, cap1, capa, capb),
        out_shape=jax.ShapeDtypeStruct((1024, 1024), bf16),
        in_specs=[anywhere] * 8,
        out_specs=anywhere,
        scratch_shapes=[
            pltpu.SMEM((192,), jnp.int32),
            pltpu.SMEM((16, 16), jnp.int32),
            pltpu.SMEM((16, 16), jnp.int32),
            pltpu.SMEM((1,), jnp.float32),
            pltpu.SMEM((1,), jnp.float32),
            pltpu.VMEM((1, 1024), jnp.float32),
            *[pltpu.VMEM((32, 2, HALF, 128), bf16)] * 2,
            *[pltpu.VMEM((8, 2, TILE, 128), bf16)] * 2,
            *[pltpu.VMEM((4, cap1, TILE, 128), bf16)] * 2,
            *[pltpu.VMEM((2, 2, capa + 1, HALF, 128), bf16)] * 4,
            *[pltpu.VMEM((capb + 1, TILE, 128), bf16)] * 8,
            pltpu.VMEM((1024, 4096), bf16),
            pltpu.VMEM((1024, 4096), bf16),
            pltpu.VMEM((1024, 1024), jnp.float32),
            pltpu.VMEM((4, 1024, 256), bf16),
            pltpu.VMEM((1024, 1024), jnp.float32),
            pltpu.VMEM((1024, 1024), bf16),
            dma((6,)),
            dma((2,)), dma((2,)), dma((2,)), dma((2,)),
            dma((3, 2, 4)), dma((3, 2, 4)), dma((4, 2)), dma((4, 2)), dma((8,)),
        ],
        compiler_params=pltpu.CompilerParams(
            collective_id=level + 1, has_side_effects=True, vmem_limit_bytes=60 << 20
        ),
    )(tab, mask_amp, mask_int, occ_i, occ_j, energy, amp, integ)


def per_device(
    amplitudes, cycle_integrals, mask_amp, mask_int, occupied_i, occupied_j, virtual_energy
):
    tab, level = tables(mask_amp, mask_int)
    branches = [functools.partial(contract, k) for k in range(len(LEVELS))]
    update = lax.switch(
        level[0], branches, tab, mask_amp, mask_int, occupied_i, occupied_j,
        virtual_energy.reshape(1, -1), amplitudes, cycle_integrals,
    )
    return update[None, None]


def solution(mesh):
    in_specs = (
        P(None, None, "row", "col"),
        P(None, None, "row", "col"),
        P(),
        P(),
        P("row"),
        P("col"),
        P(),
    )
    out_specs = P("row", "col", None, None)
    return jax.shard_map(
        per_device, mesh=mesh, in_specs=in_specs, out_specs=out_specs, check_vma=False
    )
```

```python
import functools

import jax
import jax.numpy as jnp
from jax import lax
from jax.experimental import pallas as pl
from jax.experimental.pallas import tpu as pltpu
from jax.sharding import PartitionSpec as P

TILE = 64
HALF = 32
MESH = pl.DeviceIdType.MESH

LEVELS = ((9, 26, 24), (10, 28, 26), (12, 34, 31), (16, 64, 64))


def place():
    row = lax.axis_index("row")
    col = lax.axis_index("col")
    core = col % 2
    z, y = row // 4, row % 4
    p = (1 - core) * y + core * z
    q = (1 - core) * z + core * y
    return row, col, col // 2, core, p, q


def row_at(core, p, q):
    return (p * 4 + q) * core + (q * 4 + p) * (1 - core)


def table_kernel(mask_a, mask_b, tab, level):
    row, col, x, core, p, q = place()

    def clear(t, _):
        for k in range(16):
            tab[t * 16 + k] = 0
        return 0

    lax.fori_loop(0, 12, clear, 0)

    def scan_a(a, carry):
        count, totals = carry[0], list(carry[1:])
        for cc in range(4):
            tab[count] = ((cc // 2) * 16 + a) * 2 + cc % 2
            count += mask_a[a, 4 * x + cc]
        for g in range(4):
            for cc in range(4):
                totals[g] += mask_a[a, 4 * g + cc]
        return (count, *totals)

    zero = jnp.int32(0)
    most_a = functools.reduce(jnp.maximum, lax.fori_loop(0, 16, scan_a, (zero,) * 5)[1:])

    def scan_row(c, count):
        tab[64 + count] = c
        return count + mask_b[row, c]

    lax.fori_loop(0, 16, scan_row, zero, unroll=True)

    def scan_b(g, carry):
        most_row, most_z, by_y = carry[0], carry[1], list(carry[2:])
        total = zero
        for k in range(4):
            count = zero
            for c in range(16):
                count += mask_b[4 * g + k, c]
            most_row = jnp.maximum(most_row, count)
            by_y[k] += count
            total += count
        return (most_row, jnp.maximum(most_z, total), *by_y)

    most_row, most_z, *by_y = lax.fori_loop(0, 4, scan_b, (zero,) * 6)
    most_b = functools.reduce(jnp.maximum, by_y, most_z)

    def scan_pool(k, count):
        rank = zero
        here = row_at(core, k, q)
        for c in range(16):
            tab[128 + count] = k * 16 + rank
            bit = mask_b[here, c]
            count += bit
            rank += bit
        return count

    lax.fori_loop(0, 4, scan_pool, zero)

    found = zero
    for c1, ca, cb in LEVELS[:-1]:
        found += ((most_row > c1) | (most_a > ca) | (most_b > cb)).astype(jnp.int32)
    level[0] = found


def tables(mask_amp, mask_int):
    smem = pl.BlockSpec(memory_space=pltpu.SMEM)
    return pl.pallas_call(
        table_kernel,
        out_shape=(jax.ShapeDtypeStruct((192,), jnp.int32), jax.ShapeDtypeStruct((1,), jnp.int32)),
        in_specs=[smem, smem],
        out_specs=(smem, smem),
    )(mask_amp, mask_int)


def comm_kernel(
    cap1, capa, capb, tab_in, mask_a_in, mask_b_in, occ_i_in, occ_j_in, energy_in, amp, integ, out,
    tab, mask_a, mask_b, occ_i, occ_j, energy, slots,
    ra0, ra1, rb0, rb1, b10, b11, ga0, ga1, ga2, ga3, gb0, gb1, gb2, gb3, gb4, gb5, gb6, gb7,
    acc, narrow, inverse, staged, small_sem,
    a1_send, a1_recv, b1_send, b1_recv, ring_send, ring_recv, sib_send, sib_recv, out_sem,
):
    recv_a, recv_b, grp_b1 = (ra0, ra1), (rb0, rb1), (b10, b11)
    grp_a, grp_b = (ga0, ga1, ga2, ga3), ((gb0, gb1), (gb2, gb3), (gb4, gb5), (gb6, gb7))
    row, col, x, core, p, q = place()
    sibling = (row, 2 * x + 1 - core)

    barrier = pltpu.get_barrier_semaphore()

    def signal(target):
        pl.semaphore_signal(barrier, inc=1, device_id=target, device_id_type=MESH)

    for d in range(1, 16):
        for cc in range(2):
            signal(((row + d) % 16, 2 * x + cc))
    for d in range(1, 4):
        for cc in range(2):
            signal((row, 2 * ((x + d) % 4) + cc))
    signal(sibling)
    small = [
        pltpu.make_async_copy(src, dst, small_sem.at[n]) for n, (src, dst) in enumerate((
            (tab_in, tab), (mask_a_in, mask_a), (mask_b_in, mask_b),
            (occ_i_in, occ_i), (occ_j_in, occ_j), (energy_in, energy),
        ))
    ]
    for copy in small:
        copy.start()
    pl.semaphore_wait(barrier, 37)

    def b1_copy(d, h):
        target = (col + d) % 8
        return pltpu.make_async_remote_copy(
            src_ref=integ.at[pl.ds(2 * h, 2), target], dst_ref=recv_b[h].at[col],
            send_sem=b1_send.at[h], recv_sem=b1_recv.at[h],
            device_id=(row, target), device_id_type=MESH,
        )

    def a1_copy(d, cc, h):
        target = (row + d) % 16
        return pltpu.make_async_remote_copy(
            src_ref=amp.at[target, pl.ds(2 * cc, 2), pl.ds(h * HALF, HALF)],
            dst_ref=recv_a[h].at[core * 16 + row],
            send_sem=a1_send.at[h], recv_sem=a1_recv.at[h],
            device_id=(target, 2 * x + cc), device_id_type=MESH,
        )

    a1_targets = [(d, cc) for d in range(1, 16) for cc in range(2)]
    for h in range(2):
        for d in range(1, 8):
            b1_copy(d, h).start()
        pltpu.make_async_copy(
            integ.at[pl.ds(2 * h, 2), col], recv_b[h].at[col], b1_recv.at[h]
        ).start()
        for d, cc in a1_targets:
            a1_copy(d, cc, h).start()
        a1_copy(0, 1 - core, h).start()
        pltpu.make_async_copy(
            amp.at[row, pl.ds(2 * core, 2), pl.ds(h * HALF, HALF)],
            recv_a[h].at[core * 16 + row], a1_recv.at[h],
        ).start()

    for g in range(4):
        grp_a[g][:, :, capa] = jnp.zeros((2, 2, HALF, 128), jnp.bfloat16)
        for h in range(2):
            grp_b[g][h][capb] = jnp.zeros((TILE, 128), jnp.bfloat16)

    def mixed(first, second, parity):
        side = lax.broadcasted_iota(jnp.int32, first.shape, 1) // TILE
        turned = pltpu.roll(second.astype(jnp.float32), TILE, 1)
        return jnp.where(side == parity, first.astype(jnp.float32), turned).astype(jnp.bfloat16)

    class Ring:
        def __init__(self, which, view, pos, cap, target_of, absolute=False):
            right, left, cut = (pos + 1) % 4, (pos + 3) % 4, cap // 2

            def copy(h, k, src, dst, to, s, e):
                if absolute:
                    src = dst = (pos + src) % 4
                return pltpu.make_async_remote_copy(
                    src_ref=view(h, src, s, e), dst_ref=view(h, dst, s, e),
                    send_sem=ring_send.at[which, h, k], recv_sem=ring_recv.at[which, h, k],
                    device_id=target_of(to), device_id_type=MESH,
                )

            self.copies = [(
                copy(h, 0, 0, 3, right, 0, cap), copy(h, 1, 0, 1, left, 0, cap),
                copy(h, 2, 3, 2, right, 0, cut), copy(h, 3, 1, 2, left, cut, cap),
            ) for h in range(2)]

        def start(self, h):
            self.copies[h][0].start()
            self.copies[h][1].start()

        def forward(self, h):
            for k in range(2):
                self.copies[h][k].wait_recv()
                self.copies[h][2 + k].start()

        def wait_opposite(self, h):
            self.copies[h][2].wait_recv()
            self.copies[h][3].wait_recv()

        def wait_sends(self):
            for h in range(2):
                for c in self.copies[h]:
                    c.wait_send()

    ring_b1 = Ring(0, lambda h, at, s, e: grp_b1[h].at[at, pl.ds(s, e - s)], p, cap1,
                   lambda to: (row_at(core, to, q), col), absolute=True)
    ring_b2 = Ring(1, lambda h, g, s, e: grp_b[g][h].at[pl.ds(s, e - s)], q, capb,
                   lambda to: (row_at(core, p, to), col))
    ring_a = Ring(2, lambda h, g, s, e: grp_a[g].at[core, h, pl.ds(s, e - s)], x, capa,
                  lambda to: (row, 2 * to + core))

    def sib_copy(g, h):
        ref = grp_a[g].at[core, h, pl.ds(0, capa)]
        return pltpu.make_async_remote_copy(
            src_ref=ref, dst_ref=ref, send_sem=sib_send.at[g, h], recv_sem=sib_recv.at[g, h],
            device_id=sibling, device_id_type=MESH,
        )

    def sib_wait(g):
        for h in range(2):
            there = grp_a[g].at[1 - core, h, pl.ds(0, capa)]
            pltpu.make_async_copy(there, there, sib_recv.at[g, h]).wait()

    def find_slots(rel):
        ga, gb = (x + rel) % 4, (q + rel) % 4

        def amplitudes(a, count):
            for cc in range(4):
                bit = mask_a[a, 4 * ga + cc]
                slots[rel * 64 + a * 4 + cc] = jnp.where(bit > 0, count, capa)
                count += bit
            return count

        def integrals(k, count):
            here = row_at(core, k, gb)
            for c in range(16):
                bit = mask_b[here, c]
                slots[256 + rel * 64 + k * 16 + c] = jnp.where(bit > 0, count, capb)
                count += bit
            return count

        lax.fori_loop(0, 16, amplitudes, jnp.int32(0))
        lax.fori_loop(0, 4, integrals, jnp.int32(0))

    by_place = (0, 3, 1, 2)

    def packed_rows(rel, kp, places):
        lines = []
        for k in range(4):
            tiles = []
            for place_a in range(places[0], places[0] + places[1]):
                group = (x + by_place[place_a]) % 4
                for cc in range(4):
                    tiles.append(grp_b[rel][kp][slots[256 + rel * 64 + k * 16 + 4 * group + cc]])
            lines.append(jnp.concatenate(tiles, axis=1))
        return lines

    def packed_tall(t, kp, places):
        lines = []
        for a in range(8):
            for h in range(2):
                tiles = []
                for place_a in range(places[0], places[0] + places[1]):
                    rel = by_place[place_a]
                    for cc in range(4):
                        tiles.append(grp_a[rel][kp, h, slots[rel * 64 + (t * 8 + a) * 4 + cc]])
                lines.append(jnp.concatenate(tiles, axis=1))
        return jnp.concatenate(lines, axis=0)

    def by_rows(done, columns, pairs, places):
        def body(t, _):
            rows = pl.ds(t * 512, 512)
            total = None
            for kp in pairs:
                lines = []
                for place_b in range(columns[0] // 256, (columns[0] + columns[1]) // 256):
                    lines += packed_rows(by_place[place_b], kp, places)
                part = lax.dot_general(
                    packed_tall(t, kp, places), jnp.concatenate(lines, axis=0),
                    (((1,), (1,)), ((), ())), preferred_element_type=jnp.float32,
                )
                total = part if total is None else total + part
            done(rows, pl.ds(*columns), total)
            return 0

        lax.fori_loop(0, 2, body, 0)

    def put(rows, lanes, value):
        acc[rows, lanes] = value

    def add(rows, lanes, value):
        acc[rows, lanes] += value

    def pack_b(h):
        def body(s, _):
            e = tab[64 + s]
            grp_b1[h][p, s] = mixed(recv_b[h][e // 2, 0], recv_b[h][e // 2, 1], e % 2)
            return 0

        lax.fori_loop(0, cap1, body, 0)

    def pack_a(h):
        def body(s, _):
            e = tab[s]
            grp_a[0][core, h, s] = mixed(recv_a[h][e // 2, 0], recv_a[h][e // 2, 1], e % 2)
            return 0

        lax.fori_loop(0, capa, body, 0)

    def pool_b(h):
        def body(s, _):
            e = tab[128 + s]
            grp_b[0][h][s] = grp_b1[h][e // 16, e % 16]
            return 0

        lax.fori_loop(0, capb, body, 0)

    def invert(t, _):
        rows = pl.ds(t * 128, 128)
        down = jnp.transpose(jnp.broadcast_to(energy[:, rows], (128, 128)))
        for m in range(8):
            lanes = pl.ds(m * 128, 128)
            inverse[rows, lanes] = 1.0 / (down + energy[:, lanes] - occ_i[0] - occ_j[0])
        return 0

    def emit(rows, m, value):
        lanes = pl.ds(pl.multiple_of(m * 128, 128), 128)
        staged[rows, lanes] = (value * inverse[rows, lanes]).astype(jnp.bfloat16)

    def out_copy(m):
        lanes = pl.ds(pl.multiple_of(m * 128, 128), 128)
        return pltpu.make_async_copy(staged.at[:, lanes], out.at[:, lanes], out_sem.at[m])

    def finish_group(g):
        def body(t, _):
            rows = pl.ds(t * 128, 128)
            for s in range(2):
                emit(rows, 2 * g + s, narrow[g, rows, pl.ds(s * 128, 128)].astype(jnp.float32))
            return 0

        lax.fori_loop(0, 8, body, 0)
        for s in range(2):
            out_copy(2 * g + s).start()

    lower = lax.broadcasted_iota(jnp.int32, (128, 128), 1) < TILE

    def finish_pair(h):
        def body(t, _):
            rows = pl.ds(t * 128, 128)
            for k in range(4):
                one, two = [
                    narrow[2 * h + s, rows, pl.ds((k // 2) * 128, 128)].astype(jnp.float32) for s in range(2)
                ]
                if k % 2 == 0:
                    two = pltpu.roll(two, TILE, 1)
                else:
                    one = pltpu.roll(one, TILE, 1)
                emit(rows, 2 * k + h, jnp.where(lower, one, two))
            return 0

        lax.fori_loop(0, 8, body, 0)
        for k in range(4):
            out_copy(2 * k + h).start()

    for copy in small:
        copy.wait()
    for rel in range(4):
        find_slots(rel)
    lax.fori_loop(0, 8, invert, 0)

    for h in range(2):
        pltpu.make_async_copy(recv_b[h], recv_b[h], b1_recv.at[h]).wait()
        pack_b(h)
        ring_b1.start(h)

    for h in range(2):
        pltpu.make_async_copy(recv_a[h], recv_a[h], a1_recv.at[h]).wait()
        pack_a(h)
        ring_a.start(h)
        sib_copy(0, h).start()
        ring_b1.forward(h)

    for h in range(2):
        ring_b1.wait_opposite(h)
        pool_b(h)
        ring_b2.start(h)
        ring_a.forward(h)
        sib_copy(3, h).start()
        sib_copy(1, h).start()

    sib_wait(0)
    by_rows(put, (0, 256), (0, 1), (0, 1))

    ring_b2.forward(0)
    sib_wait(3)
    sib_wait(1)
    by_rows(add, (0, 256), (0, 1), (1, 2))
    by_rows(put, (256, 512), (0,), (0, 3))

    ring_b2.forward(1)
    for h in range(2):
        ring_a.wait_opposite(h)
        sib_copy(2, h).start()
    by_rows(add, (256, 512), (1,), (0, 3))

    sib_wait(2)

    def finish_three(rows, lanes, value):
        total = (acc[rows, lanes] + value).astype(jnp.bfloat16)
        for pos, rel in enumerate((0, 3, 1)):
            narrow[(q + rel) % 4, rows] = total[:, pos * 256:(pos + 1) * 256]

    by_rows(finish_three, (0, 768), (0, 1), (3, 1))

    opposite = (q + 2) % 4

    ring_b2.wait_opposite(0)
    by_rows(put, (768, 256), (0,), (0, 4))

    @pl.when(core == 0)
    def _():
        for rel in (0, 3, 1):
            finish_group((q + rel) % 4)

    @pl.when(core == 1)
    def _():
        finish_pair(1 - opposite // 2)

    ring_b2.wait_opposite(1)

    def finish_last(rows, lanes, value):
        narrow[opposite, rows] = (acc[rows, lanes] + value).astype(jnp.bfloat16)

    by_rows(finish_last, (768, 256), (1,), (0, 4))

    @pl.when(core == 0)
    def _():
        finish_group(opposite)

    @pl.when(core == 1)
    def _():
        finish_pair(opposite // 2)

    for h in range(2):
        for d in range(1, 8):
            b1_copy(d, h).wait_send()
        for d, cc in a1_targets:
            a1_copy(d, cc, h).wait_send()
        a1_copy(0, 1 - core, h).wait_send()
        for g in range(4):
            sib_copy(g, h).wait_send()
    for ring in (ring_b1, ring_b2, ring_a):
        ring.wait_sends()
    for m in range(8):
        out_copy(m).wait()


def contract(level, tab, mask_amp, mask_int, occ_i, occ_j, energy, amp, integ):
    cap1, capa, capb = LEVELS[level]
    bf16 = jnp.bfloat16
    dma = pltpu.SemaphoreType.DMA
    anywhere = pl.BlockSpec(memory_space=pl.ANY)
    return pl.pallas_call(
        functools.partial(comm_kernel, cap1, capa, capb),
        out_shape=jax.ShapeDtypeStruct((1024, 1024), bf16),
        in_specs=[anywhere] * 8,
        out_specs=anywhere,
        scratch_shapes=[
            pltpu.SMEM((192,), jnp.int32),
            pltpu.SMEM((16, 16), jnp.int32),
            pltpu.SMEM((16, 16), jnp.int32),
            pltpu.SMEM((1,), jnp.float32),
            pltpu.SMEM((1,), jnp.float32),
            pltpu.VMEM((1, 1024), jnp.float32),
            pltpu.SMEM((512,), jnp.int32),
            *[pltpu.VMEM((32, 2, HALF, 128), bf16)] * 2,
            *[pltpu.VMEM((8, 2, TILE, 128), bf16)] * 2,
            *[pltpu.VMEM((4, cap1, TILE, 128), bf16)] * 2,
            *[pltpu.VMEM((2, 2, capa + 1, HALF, 128), bf16)] * 4,
            *[pltpu.VMEM((capb + 1, TILE, 128), bf16)] * 8,
            pltpu.VMEM((1024, 1024), jnp.float32),
            pltpu.VMEM((4, 1024, 256), bf16),
            pltpu.VMEM((1024, 1024), jnp.float32),
            pltpu.VMEM((1024, 1024), bf16),
            dma((6,)),
            dma((2,)), dma((2,)), dma((2,)), dma((2,)),
            dma((3, 2, 4)), dma((3, 2, 4)), dma((4, 2)), dma((4, 2)), dma((8,)),
        ],
        compiler_params=pltpu.CompilerParams(
            collective_id=level + 1, has_side_effects=True, vmem_limit_bytes=60 << 20
        ),
    )(tab, mask_amp, mask_int, occ_i, occ_j, energy, amp, integ)


def per_device(
    amplitudes, cycle_integrals, mask_amp, mask_int, occupied_i, occupied_j, virtual_energy
):
    tab, level = tables(mask_amp, mask_int)
    branches = [functools.partial(contract, k) for k in range(len(LEVELS))]
    update = lax.switch(
        level[0], branches, tab, mask_amp, mask_int, occupied_i, occupied_j,
        virtual_energy.reshape(1, -1), amplitudes, cycle_integrals,
    )
    return update[None, None]


def solution(mesh):
    in_specs = (
        P(None, None, "row", "col"),
        P(None, None, "row", "col"),
        P(),
        P(),
        P("row"),
        P("col"),
        P(),
    )
    out_specs = P("row", "col", None, None)
    return jax.shard_map(
        per_device, mesh=mesh, in_specs=in_specs, out_specs=out_specs, check_vma=False
    )
```

```python
import functools

import jax
import jax.numpy as jnp
from jax import lax
from jax.experimental import pallas as pl
from jax.experimental.pallas import tpu as pltpu
from jax.sharding import PartitionSpec as P

TILE = 64
HALF = 32
MESH = pl.DeviceIdType.MESH

LEVELS = ((8, 25, 24), (9, 27, 27), (12, 34, 31), (16, 64, 64))


def place():
    row = lax.axis_index("row")
    col = lax.axis_index("col")
    core = col % 2
    z, y = row // 4, row % 4
    p = (1 - core) * y + core * z
    q = (1 - core) * z + core * y
    return row, col, col // 2, core, p, q


def row_at(core, p, q):
    return (p * 4 + q) * core + (q * 4 + p) * (1 - core)


def table_kernel(mask_a_in, mask_b_in, tab, level, mask_a, mask_b, vec_a, vec_b, sem):
    row, col, x, core, p, q = place()
    copies = [
        pltpu.make_async_copy(src, dst, sem.at[n]) for n, (src, dst) in enumerate((
            (mask_a_in, vec_a), (mask_b_in, vec_b), (mask_a_in, mask_a), (mask_b_in, mask_b),
        ))
    ]
    for copy in copies:
        copy.start()

    def clear(t, _):
        for k in range(64):
            tab[t * 64 + k] = 0
        return 0

    lax.fori_loop(0, 3, clear, 0)
    for copy in copies:
        copy.wait()

    tiles_a, tiles_b = vec_a[...].astype(jnp.float32), vec_b[...].astype(jnp.float32)
    down = lax.broadcasted_iota(jnp.int32, (16, 16), 0)
    along = lax.broadcasted_iota(jnp.int32, (16, 16), 1)

    def most(tiles, group):
        totals = [jnp.sum(jnp.where(group == g, tiles, 0.0)) for g in range(4)]
        return functools.reduce(jnp.maximum, totals)

    most_a = most(tiles_a, along // 4)
    most_b = jnp.maximum(most(tiles_b, down // 4), most(tiles_b, down % 4))
    most_row = jnp.max(jnp.sum(tiles_b, axis=1, keepdims=True))

    def scan_a(t, count):
        for a in range(4):
            for cc in range(4):
                tab[count] = ((cc // 2) * 16 + 4 * t + a) * 2 + cc % 2
                count += mask_a[4 * t + a, 4 * x + cc]
        return count

    zero = jnp.int32(0)
    lax.fori_loop(0, 4, scan_a, zero)

    count = zero
    for c in range(16):
        tab[64 + count] = c
        count += mask_b[row, c]

    def scan_pool(k, count):
        rank = zero
        here = row_at(core, k, q)
        for c in range(16):
            tab[128 + count] = k * 16 + rank
            bit = mask_b[here, c]
            count += bit
            rank += bit
        return count

    lax.fori_loop(0, 4, scan_pool, zero)

    found = zero
    for c1, ca, cb in LEVELS[:-1]:
        found += ((most_row > c1) | (most_a > ca) | (most_b > cb)).astype(jnp.int32)
    level[0] = found


def tables(mask_amp, mask_int):
    smem = pl.BlockSpec(memory_space=pltpu.SMEM)
    anywhere = pl.BlockSpec(memory_space=pl.ANY)
    small = (16, 16)
    return pl.pallas_call(
        table_kernel,
        out_shape=(jax.ShapeDtypeStruct((192,), jnp.int32), jax.ShapeDtypeStruct((1,), jnp.int32)),
        in_specs=[anywhere, anywhere],
        out_specs=(smem, smem),
        scratch_shapes=[
            pltpu.SMEM(small, jnp.int32), pltpu.SMEM(small, jnp.int32),
            pltpu.VMEM(small, jnp.int32), pltpu.VMEM(small, jnp.int32),
            pltpu.SemaphoreType.DMA((4,)),
        ],
    )(mask_amp, mask_int)


def comm_kernel(
    cap1, capa, capb, tab_in, mask_a_in, mask_b_in, occ_i_in, occ_j_in, energy_in, amp, integ, out,
    tab, mask_a, mask_b, occ_i, occ_j, energy, slots,
    ra0, ra1, rb0, rb1, b10, b11, ga0, ga1, ga2, ga3, gb0, gb1, gb2, gb3, gb4, gb5, gb6, gb7,
    acc, narrow, inverse, staged, small_sem,
    a1_send, a1_recv, b1_send, b1_recv, ring_send, ring_recv, sib_send, sib_recv, out_sem,
):
    recv_a, recv_b, grp_b1 = (ra0, ra1), (rb0, rb1), (b10, b11)
    grp_a, grp_b = (ga0, ga1, ga2, ga3), ((gb0, gb1), (gb2, gb3), (gb4, gb5), (gb6, gb7))
    row, col, x, core, p, q = place()
    sibling = (row, 2 * x + 1 - core)

    barrier = pltpu.get_barrier_semaphore()

    def signal(target):
        pl.semaphore_signal(barrier, inc=1, device_id=target, device_id_type=MESH)

    for d in range(1, 16):
        for cc in range(2):
            signal(((row + d) % 16, 2 * x + cc))
    for d in range(1, 4):
        for cc in range(2):
            signal((row, 2 * ((x + d) % 4) + cc))
    signal(sibling)
    small = [
        pltpu.make_async_copy(src, dst, small_sem.at[n]) for n, (src, dst) in enumerate((
            (tab_in, tab), (mask_a_in, mask_a), (mask_b_in, mask_b),
            (occ_i_in, occ_i), (occ_j_in, occ_j), (energy_in, energy),
        ))
    ]
    for copy in small:
        copy.start()
    pl.semaphore_wait(barrier, 37)

    def b1_copy(d, h):
        target = (col + d) % 8
        return pltpu.make_async_remote_copy(
            src_ref=integ.at[pl.ds(2 * h, 2), target], dst_ref=recv_b[h].at[col],
            send_sem=b1_send.at[h], recv_sem=b1_recv.at[h],
            device_id=(row, target), device_id_type=MESH,
        )

    def a1_copy(d, cc, h):
        target = (row + d) % 16
        return pltpu.make_async_remote_copy(
            src_ref=amp.at[target, pl.ds(2 * cc, 2), pl.ds(h * HALF, HALF)],
            dst_ref=recv_a[h].at[core * 16 + row],
            send_sem=a1_send.at[h], recv_sem=a1_recv.at[h],
            device_id=(target, 2 * x + cc), device_id_type=MESH,
        )

    a1_targets = [(d, cc) for d in range(1, 16) for cc in range(2)]
    for h in range(2):
        for d in range(1, 8):
            b1_copy(d, h).start()
        pltpu.make_async_copy(
            integ.at[pl.ds(2 * h, 2), col], recv_b[h].at[col], b1_recv.at[h]
        ).start()
        for d, cc in a1_targets:
            a1_copy(d, cc, h).start()
        a1_copy(0, 1 - core, h).start()
        pltpu.make_async_copy(
            amp.at[row, pl.ds(2 * core, 2), pl.ds(h * HALF, HALF)],
            recv_a[h].at[core * 16 + row], a1_recv.at[h],
        ).start()

    for g in range(4):
        grp_a[g][:, :, capa] = jnp.zeros((2, 2, HALF, 128), jnp.bfloat16)
        for h in range(2):
            grp_b[g][h][capb] = jnp.zeros((TILE, 128), jnp.bfloat16)

    def mixed(first, second, parity):
        side = lax.broadcasted_iota(jnp.int32, first.shape, 1) // TILE
        turned = pltpu.roll(second.astype(jnp.float32), TILE, 1)
        return jnp.where(side == parity, first.astype(jnp.float32), turned).astype(jnp.bfloat16)

    class Ring:
        def __init__(self, which, view, pos, cap, target_of, absolute=False):
            right, left, cut = (pos + 1) % 4, (pos + 3) % 4, cap // 2

            def copy(h, k, src, dst, to, s, e):
                if absolute:
                    src = dst = (pos + src) % 4
                return pltpu.make_async_remote_copy(
                    src_ref=view(h, src, s, e), dst_ref=view(h, dst, s, e),
                    send_sem=ring_send.at[which, h, k], recv_sem=ring_recv.at[which, h, k],
                    device_id=target_of(to), device_id_type=MESH,
                )

            self.copies = [(
                copy(h, 0, 0, 3, right, 0, cap), copy(h, 1, 0, 1, left, 0, cap),
                copy(h, 2, 3, 2, right, 0, cut), copy(h, 3, 1, 2, left, cut, cap),
            ) for h in range(2)]

        def start(self, h):
            self.copies[h][0].start()
            self.copies[h][1].start()

        def forward(self, h):
            for k in range(2):
                self.copies[h][k].wait_recv()
                self.copies[h][2 + k].start()

        def wait_opposite(self, h):
            self.copies[h][2].wait_recv()
            self.copies[h][3].wait_recv()

        def wait_sends(self):
            for h in range(2):
                for c in self.copies[h]:
                    c.wait_send()

    ring_b1 = Ring(0, lambda h, at, s, e: grp_b1[h].at[at, pl.ds(s, e - s)], p, cap1,
                   lambda to: (row_at(core, to, q), col), absolute=True)
    ring_b2 = Ring(1, lambda h, g, s, e: grp_b[g][h].at[pl.ds(s, e - s)], q, capb,
                   lambda to: (row_at(core, p, to), col))
    ring_a = Ring(2, lambda h, g, s, e: grp_a[g].at[core, h, pl.ds(s, e - s)], x, capa,
                  lambda to: (row, 2 * to + core))

    def sib_copy(g, h):
        ref = grp_a[g].at[core, h, pl.ds(0, capa)]
        return pltpu.make_async_remote_copy(
            src_ref=ref, dst_ref=ref, send_sem=sib_send.at[g, h], recv_sem=sib_recv.at[g, h],
            device_id=sibling, device_id_type=MESH,
        )

    def sib_wait(g):
        for h in range(2):
            there = grp_a[g].at[1 - core, h, pl.ds(0, capa)]
            pltpu.make_async_copy(there, there, sib_recv.at[g, h]).wait()

    def find_slots(rel):
        ga, gb = (x + rel) % 4, (q + rel) % 4

        def amplitudes(a, count):
            for cc in range(4):
                bit = mask_a[a, 4 * ga + cc]
                slots[rel * 64 + a * 4 + cc] = jnp.where(bit > 0, count, capa)
                count += bit
            return count

        def integrals(k, count):
            here = row_at(core, k, gb)
            for c in range(16):
                bit = mask_b[here, c]
                slots[256 + rel * 64 + k * 16 + c] = jnp.where(bit > 0, count, capb)
                count += bit
            return count

        lax.fori_loop(0, 16, amplitudes, jnp.int32(0))
        lax.fori_loop(0, 4, integrals, jnp.int32(0))

    by_place = (0, 3, 1, 2)

    def packed_rows(rel, kp, places):
        lines = []
        for k in range(4):
            tiles = []
            for place_a in range(places[0], places[0] + places[1]):
                group = (x + by_place[place_a]) % 4
                for cc in range(4):
                    tiles.append(grp_b[rel][kp][slots[256 + rel * 64 + k * 16 + 4 * group + cc]])
            lines.append(jnp.concatenate(tiles, axis=1))
        return lines

    def packed_tall(t, kp, places):
        lines = []
        for a in range(8):
            for h in range(2):
                tiles = []
                for place_a in range(places[0], places[0] + places[1]):
                    rel = by_place[place_a]
                    for cc in range(4):
                        tiles.append(grp_a[rel][kp, h, slots[rel * 64 + (t * 8 + a) * 4 + cc]])
                lines.append(jnp.concatenate(tiles, axis=1))
        return jnp.concatenate(lines, axis=0)

    def by_rows(done, columns, pairs, places):
        def body(t, _):
            rows = pl.ds(t * 512, 512)
            total = None
            for kp in pairs:
                lines = []
                for place_b in range(columns[0] // 256, (columns[0] + columns[1]) // 256):
                    lines += packed_rows(by_place[place_b], kp, places)
                part = lax.dot_general(
                    packed_tall(t, kp, places), jnp.concatenate(lines, axis=0),
                    (((1,), (1,)), ((), ())), preferred_element_type=jnp.float32,
                )
                total = part if total is None else total + part
            done(rows, pl.ds(*columns), total)
            return 0

        lax.fori_loop(0, 2, body, 0)

    def put(rows, lanes, value):
        acc[rows, lanes] = value

    def add(rows, lanes, value):
        acc[rows, lanes] += value

    def pack_b(h):
        def body(s, _):
            e = tab[64 + s]
            grp_b1[h][p, s] = mixed(recv_b[h][e // 2, 0], recv_b[h][e // 2, 1], e % 2)
            return 0

        lax.fori_loop(0, cap1, body, 0)

    def pack_a(h):
        def body(s, _):
            e = tab[s]
            grp_a[0][core, h, s] = mixed(recv_a[h][e // 2, 0], recv_a[h][e // 2, 1], e % 2)
            return 0

        lax.fori_loop(0, capa, body, 0)

    def pool_b(h):
        def body(s, _):
            e = tab[128 + s]
            grp_b[0][h][s] = grp_b1[h][e // 16, jnp.minimum(e % 16, cap1 - 1)]
            return 0

        lax.fori_loop(0, capb, body, 0)

    def invert(t, _):
        rows = pl.ds(t * 128, 128)
        down = jnp.transpose(jnp.broadcast_to(energy[:, rows], (128, 128)))
        for m in range(8):
            lanes = pl.ds(m * 128, 128)
            inverse[rows, lanes] = 1.0 / (down + energy[:, lanes] - occ_i[0] - occ_j[0])
        return 0

    def emit(rows, m, value):
        lanes = pl.ds(pl.multiple_of(m * 128, 128), 128)
        staged[rows, lanes] = (value * inverse[rows, lanes]).astype(jnp.bfloat16)

    def out_copy(m):
        lanes = pl.ds(pl.multiple_of(m * 128, 128), 128)
        return pltpu.make_async_copy(staged.at[:, lanes], out.at[:, lanes], out_sem.at[m])

    def finish_group(g):
        def body(t, _):
            rows = pl.ds(t * 128, 128)
            for s in range(2):
                emit(rows, 2 * g + s, narrow[g, rows, pl.ds(s * 128, 128)].astype(jnp.float32))
            return 0

        lax.fori_loop(0, 8, body, 0)
        for s in range(2):
            out_copy(2 * g + s).start()

    lower = lax.broadcasted_iota(jnp.int32, (128, 128), 1) < TILE

    def finish_pair(h):
        def body(t, _):
            rows = pl.ds(t * 128, 128)
            for k in range(4):
                one, two = [
                    narrow[2 * h + s, rows, pl.ds((k // 2) * 128, 128)].astype(jnp.float32) for s in range(2)
                ]
                if k % 2 == 0:
                    two = pltpu.roll(two, TILE, 1)
                else:
                    one = pltpu.roll(one, TILE, 1)
                emit(rows, 2 * k + h, jnp.where(lower, one, two))
            return 0

        lax.fori_loop(0, 8, body, 0)
        for k in range(4):
            out_copy(2 * k + h).start()

    for copy in small:
        copy.wait()
    for rel in range(4):
        find_slots(rel)
    lax.fori_loop(0, 8, invert, 0)

    for h in range(2):
        pltpu.make_async_copy(recv_b[h], recv_b[h], b1_recv.at[h]).wait()
        pack_b(h)
        ring_b1.start(h)

    for h in range(2):
        pltpu.make_async_copy(recv_a[h], recv_a[h], a1_recv.at[h]).wait()
        pack_a(h)
        ring_a.start(h)
        sib_copy(0, h).start()
        ring_b1.forward(h)

    for h in range(2):
        ring_b1.wait_opposite(h)
        pool_b(h)
        ring_b2.start(h)
        ring_a.forward(h)
        sib_copy(3, h).start()
        sib_copy(1, h).start()

    sib_wait(0)
    by_rows(put, (0, 256), (0, 1), (0, 1))

    ring_b2.forward(0)
    sib_wait(3)
    sib_wait(1)
    by_rows(add, (0, 256), (0, 1), (1, 2))
    by_rows(put, (256, 512), (0,), (0, 3))

    ring_b2.forward(1)
    for h in range(2):
        ring_a.wait_opposite(h)
        sib_copy(2, h).start()
    by_rows(add, (256, 512), (1,), (0, 3))

    sib_wait(2)

    def finish_three(rows, lanes, value):
        total = (acc[rows, lanes] + value).astype(jnp.bfloat16)
        for pos, rel in enumerate((0, 3, 1)):
            narrow[(q + rel) % 4, rows] = total[:, pos * 256:(pos + 1) * 256]

    by_rows(finish_three, (0, 768), (0, 1), (3, 1))

    opposite = (q + 2) % 4

    ring_b2.wait_opposite(0)
    by_rows(put, (768, 256), (0,), (0, 4))

    @pl.when(core == 0)
    def _():
        for rel in (0, 3, 1):
            finish_group((q + rel) % 4)

    @pl.when(core == 1)
    def _():
        finish_pair(1 - opposite // 2)

    ring_b2.wait_opposite(1)

    def finish_last(rows, lanes, value):
        narrow[opposite, rows] = (acc[rows, lanes] + value).astype(jnp.bfloat16)

    by_rows(finish_last, (768, 256), (1,), (0, 4))

    @pl.when(core == 0)
    def _():
        finish_group(opposite)

    @pl.when(core == 1)
    def _():
        finish_pair(opposite // 2)

    for h in range(2):
        for d in range(1, 8):
            b1_copy(d, h).wait_send()
        for d, cc in a1_targets:
            a1_copy(d, cc, h).wait_send()
        a1_copy(0, 1 - core, h).wait_send()
        for g in range(4):
            sib_copy(g, h).wait_send()
    for ring in (ring_b1, ring_b2, ring_a):
        ring.wait_sends()
    for m in range(8):
        out_copy(m).wait()


def contract(level, tab, mask_amp, mask_int, occ_i, occ_j, energy, amp, integ):
    cap1, capa, capb = LEVELS[level]
    bf16 = jnp.bfloat16
    dma = pltpu.SemaphoreType.DMA
    anywhere = pl.BlockSpec(memory_space=pl.ANY)
    return pl.pallas_call(
        functools.partial(comm_kernel, cap1, capa, capb),
        out_shape=jax.ShapeDtypeStruct((1024, 1024), bf16),
        in_specs=[anywhere] * 8,
        out_specs=anywhere,
        scratch_shapes=[
            pltpu.SMEM((192,), jnp.int32),
            pltpu.SMEM((16, 16), jnp.int32),
            pltpu.SMEM((16, 16), jnp.int32),
            pltpu.SMEM((1,), jnp.float32),
            pltpu.SMEM((1,), jnp.float32),
            pltpu.VMEM((1, 1024), jnp.float32),
            pltpu.SMEM((512,), jnp.int32),
            *[pltpu.VMEM((32, 2, HALF, 128), bf16)] * 2,
            *[pltpu.VMEM((8, 2, TILE, 128), bf16)] * 2,
            *[pltpu.VMEM((4, cap1, TILE, 128), bf16)] * 2,
            *[pltpu.VMEM((2, 2, capa + 1, HALF, 128), bf16)] * 4,
            *[pltpu.VMEM((capb + 1, TILE, 128), bf16)] * 8,
            pltpu.VMEM((1024, 1024), jnp.float32),
            pltpu.VMEM((4, 1024, 256), bf16),
            pltpu.VMEM((1024, 1024), jnp.float32),
            pltpu.VMEM((1024, 1024), bf16),
            dma((6,)),
            dma((2,)), dma((2,)), dma((2,)), dma((2,)),
            dma((3, 2, 4)), dma((3, 2, 4)), dma((4, 2)), dma((4, 2)), dma((8,)),
        ],
        compiler_params=pltpu.CompilerParams(
            collective_id=level + 1, has_side_effects=True, vmem_limit_bytes=60 << 20
        ),
    )(tab, mask_amp, mask_int, occ_i, occ_j, energy, amp, integ)


def per_device(
    amplitudes, cycle_integrals, mask_amp, mask_int, occupied_i, occupied_j, virtual_energy
):
    tab, level = tables(mask_amp, mask_int)
    branches = [functools.partial(contract, k) for k in range(len(LEVELS))]
    update = lax.switch(
        level[0], branches, tab, mask_amp, mask_int, occupied_i, occupied_j,
        virtual_energy.reshape(1, -1), amplitudes, cycle_integrals,
    )
    return update[None, None]


def solution(mesh):
    in_specs = (
        P(None, None, "row", "col"),
        P(None, None, "row", "col"),
        P(),
        P(),
        P("row"),
        P("col"),
        P(),
    )
    out_specs = P("row", "col", None, None)
    return jax.shard_map(
        per_device, mesh=mesh, in_specs=in_specs, out_specs=out_specs, check_vma=False
    )
```
